128 devices in a mesh: gx: 4 (over y), gy: 32 (over x, z, core).
Axes of the slice: x: 4, y: 4, z: 4, core: 2. Of those that a mesh axis runs over, the one named last changes fastest.
Arguments:
- slave_coords: float32 [3, 8388608], P(None, ('gx', 'gy')), may hold values from -6 to 6
- slave_weight: float32 [8388608], P(('gx', 'gy')), may hold values from 0.5 to 2
- master_ctrl: float32 [3, 8388608], P(None, ('gx', 'gy')), may hold values from -6 to 6
- master_wt: float32 [8388608], P(('gx', 'gy')), may hold values from 0.5 to 2
- pair_slave: int32 [81920], P(('gx', 'gy')), may hold values from 0 to 511
- pair_master: int32 [81920], P(('gx', 'gy')), may hold values from 0 to 255
- pair_count: int32 [16384], P(('gx', 'gy')), may hold values from 0 to 5, as said below
Outputs:
- slave_force: float32 [3, 8388608], P(None, ('gx', 'gy'))
- master_force: float32 [3, 8388608], P(None, ('gx', 'gy'))
The draws below stay inside these ranges and needn't reach their ends.
Inputs may be any that keep to these rules, and one draw needn't show every extreme that they name: `pair_count`: entry s * 128 + o counts the live slots from device s to owner o; in every draw some owner gets 5 live slots from every device. `pair_slave`: entries of slots that are not live are block numbers too and change nothing.
All inputs are finite; a program needn't handle non-finite values.
Results may differ from the reference program's by a relative error of at most 0.0003.
Values sent between devices are 32-bit elements; how exact they have to be, the bound alone decides.
No kernel may reach another device: no remote copies, remote signals or barrier semaphores. Data moves between devices by JAX's collectives and lax.ppermute only.
A program may use at most 64 MiB of HBM per device.

```python
import math
import jax
import jax.numpy as jnp
from jax import lax

QP = 128
CAP = 5
SB_DEV = 512
MB_DEV = 256
MP = 256
OWNERS = 128
NSP = 8388608
NMC = 8388608
SLOTS = 81920
N_GX = 4
N_GY = 32


def draw_pair_count(key, part):
    key_level, key_hot, key_first, key_second = jax.random.split(key, 4)
    level = jax.random.randint(key_level, (OWNERS,), 0, CAP + 1)
    hottest = jax.random.randint(key_hot, (), 0, OWNERS)
    is_hot = jnp.arange(OWNERS) == hottest
    level = jnp.where(is_hot, CAP, level)
    first = jax.random.randint(key_first, (OWNERS, OWNERS), 0, CAP + 1)
    second = jax.random.randint(key_second, (OWNERS, OWNERS), 0, CAP + 1)
    counts = jnp.minimum(jnp.maximum(first, second), level[None, :])
    counts = jnp.where(is_hot[None, :], CAP, counts)
    return counts.reshape(OWNERS * OWNERS).astype(jnp.int32)


def touch_ends(entries, own_key, low, high):
    longest = entries.shape.index(max(entries.shape))
    spots = []
    for shift in (0, 1):
        where = [jax.random.randint(jax.random.fold_in(own_key, axis), (), 0, length) for axis, length in enumerate(entries.shape)]
        where[longest] = (where[longest] + shift) % entries.shape[longest]
        spots.append(tuple(where))
    return entries.at[spots[0]].set(low).at[spots[1]].set(high)


def steps_of(own_key, shape, shards, low, largest):
    def one(axis_at, blocks):
        steps = jax.random.uniform(jax.random.fold_in(jax.random.fold_in(own_key, 6), axis_at), (blocks,), jnp.float32, low / len(shards), largest / len(shards))
        return jnp.repeat(jnp.exp(steps), shape[axis_at] // blocks).reshape((-1,) + (1,) * (len(shape) - axis_at - 1))

    level = one(*shards[0])
    for cut in shards[1:]:
        level = level * one(*cut)
    return level


def normal_values(stream_key, extent, width, reach, pieces=(), kind=jnp.bfloat16):
    entries = width * jax.random.normal(stream_key, extent, jnp.float32)
    if pieces:
        entries = entries * steps_of(stream_key, extent, pieces, -0.22, 0.18)
    return jnp.clip(entries, -reach, reach).astype(kind)


def setup_inputs(seed: int = 0) -> dict:
    key_list = jax.random.split(jax.random.key(seed), 8)
    slave_coords = normal_values(key_list[0], (3, NSP), 1.0, 6.0, ((1, 128),), jnp.float32)
    slave_weight = jnp.clip(jnp.exp(math.log(2.0) - 1.3862944 * jax.random.uniform(key_list[1], (NSP,), jnp.float32) ** steps_of(key_list[1], (NSP,), ((0, 128),), -0.2, 0.2)), 0.5, 2.0)
    master_ctrl = normal_values(key_list[2], (3, NMC), 1.0, 6.0, ((1, 128),), jnp.float32)
    master_wt = jnp.clip(jnp.exp(math.log(2.0) - 1.3862944 * jax.random.uniform(key_list[3], (NMC,), jnp.float32) ** steps_of(key_list[3], (NMC,), ((0, 128),), -0.2, 0.2)), 0.5, 2.0)
    pair_slave = touch_ends(jax.random.randint(key_list[4], (SLOTS,), 0, SB_DEV), jax.random.fold_in(key_list[4], 1), 0, SB_DEV - 1).astype(jnp.int32)
    pair_master = touch_ends(jax.random.randint(key_list[5], (SLOTS,), 0, MB_DEV), jax.random.fold_in(key_list[5], 1), 0, MB_DEV - 1).astype(jnp.int32)
    pair_count = draw_pair_count(jax.random.fold_in(key_list[7], 71), 0)
    return dict(slave_coords=slave_coords, slave_weight=slave_weight, master_ctrl=master_ctrl, master_wt=master_wt, pair_slave=pair_slave, pair_master=pair_master, pair_count=pair_count)


inverse_width = 1.0 / 3.0
force_gain = 0.01


def bezier_table():
    params = (jnp.arange(4, dtype=jnp.float32) + 0.5) / 4.0
    powers = jnp.arange(4, dtype=jnp.float32)
    binomial = jnp.array([1.0, 3.0, 3.0, 1.0], dtype=jnp.float32)
    bernstein = binomial[None, :] * params[:, None] ** powers[None, :] * (1.0 - params[:, None]) ** (3.0 - powers[None, :])
    return (bernstein[:, None, :, None] * bernstein[None, :, None, :]).reshape(16, 16)


def sample_blocks(blocks):
    block_count = blocks.shape[1]
    patch_count = blocks.shape[2] // 16
    basis_table = bezier_table()
    patch_grid = blocks.reshape(4, block_count, patch_count, 16)
    weights = patch_grid[3]
    numerator = jnp.einsum('jk,cnpk->cnpj', basis_table, patch_grid[:3] * weights[None], precision=lax.Precision.HIGHEST)
    denominator = jnp.einsum('jk,npk->npj', basis_table, weights, precision=lax.Precision.HIGHEST)
    samples = (numerator / denominator[None]).reshape(3, block_count, patch_count * 16)
    spread = basis_table[None, None] * weights[:, :, None, :] / denominator[..., None]
    return samples, spread


def tile_forces(points, weights, blocks):
    samples, spread = sample_blocks(blocks)
    block_count = blocks.shape[1]
    patch_count = blocks.shape[2] // 16
    differ = points[:, :, :, None] - samples[:, :, None, :]
    distance = jnp.sum(differ * differ, axis=0)
    kernel = weights[:, :, None] * jnp.exp(-distance * inverse_width) * force_gain
    weighted = kernel[None] * differ
    slave_term = jnp.sum(weighted, axis=3)
    sample_term = -jnp.sum(weighted, axis=2)
    sample_grid = sample_term.reshape(3, block_count, patch_count, 16)
    master_term = jnp.sum(spread[None] * sample_grid[..., None], axis=3)
    return slave_term, master_term.reshape(3, block_count, patch_count * 16)


def reference(slave_coords, slave_weight, master_ctrl, master_wt, pair_slave, pair_master, pair_count):
    owners = N_GX * N_GY
    slave_grid = slave_coords.reshape(3, owners * SB_DEV, QP)
    weight_grid = slave_weight.reshape(owners * SB_DEV, QP)
    master_blocks = jnp.concatenate([master_ctrl, master_wt[None, :]], axis=0).reshape(4, owners * MB_DEV, MP)
    slot_index = jnp.arange(owners * CAP, dtype=jnp.int32)
    slot_cap = slot_index % CAP
    slot_owner = slot_index // CAP
    slave_table = pair_slave.reshape(owners, owners * CAP)
    master_table = pair_master.reshape(owners, owners * CAP)
    count_table = pair_count.reshape(owners, owners)

    def one_source(carried, source):
        slave_acc, master_acc = carried
        slave_ids = (source * SB_DEV + slave_table[source]).astype(jnp.int32)
        master_ids = (slot_owner * MB_DEV + master_table[source]).astype(jnp.int32)
        live_mask = (slot_cap < count_table[source][slot_owner]).astype(jnp.float32)
        points = jnp.take(slave_grid, slave_ids, axis=1)
        weights = jnp.take(weight_grid, slave_ids, axis=0) * live_mask[:, None]
        blocks = jnp.take(master_blocks, master_ids, axis=1)
        slave_term, master_term = tile_forces(points, weights, blocks)
        slave_acc = slave_acc.at[:, slave_ids].add(slave_term)
        master_acc = master_acc.at[:, master_ids].add(master_term)
        return (slave_acc, master_acc), None

    initial = (jnp.zeros((3, owners * SB_DEV, QP), jnp.float32), jnp.zeros((3, owners * MB_DEV, MP), jnp.float32))
    (slave_acc, master_acc), unused = lax.scan(one_source, initial, jnp.arange(owners, dtype=jnp.int32))
    return slave_acc.reshape(3, owners * SB_DEV * QP), master_acc.reshape(3, owners * MB_DEV * MP)
```

```python
import math

import jax
import jax.numpy as jnp
from jax import lax
from jax.experimental import pallas as pl
from jax.experimental.pallas import tpu as pltpu
from jax.sharding import Mesh
from jax.sharding import PartitionSpec as P

QP = 128
CAP = 5
SB = 512
MB = 256
MP = 256
PEERS = 64
PER = 2 * CAP
GROUP = 4
FROWS = 32

f32 = jnp.float32
bf16 = jnp.bfloat16
SCALE = math.sqrt(2.0 * math.log2(math.e) / 3.0)
GAIN = 0.01 / SCALE

VMEM_SPEC = pl.BlockSpec(memory_space=pltpu.VMEM)
SMEM_SPEC = pl.BlockSpec(memory_space=pltpu.SMEM)


def bezier_table():
    params = (jnp.arange(4, dtype=f32) + 0.5) / 4.0
    powers = jnp.arange(4, dtype=f32)
    binomial = jnp.array([1.0, 3.0, 3.0, 1.0], dtype=f32)
    bernstein = (
        binomial[None, :]
        * params[:, None] ** powers[None, :]
        * (1.0 - params[:, None]) ** (3.0 - powers[None, :])
    )
    return (bernstein[:, None, :, None] * bernstein[None, :, None, :]).reshape(16, 16)


def dot(a, b, left, right):
    return lax.dot_general(a, b, (((left,), (right,)), ((), ())), preferred_element_type=f32)


def narrow(x):
    return x.astype(bf16).astype(f32)


def pack_kernel(ps, pm, cnt, coords, weight, out):
    lane = lax.broadcasted_iota(jnp.int32, (1, 128), 1)

    def one_peer(peer, unused):
        row = jnp.full((1, 128), -1, jnp.int32)
        for c in range(PER):
            slot = peer * PER + c
            block = ps[slot]
            out[peer, c, 0:3, :] = coords[block]
            out[peer, c, 3:4, :] = weight[pl.ds(block, 1), :]
            live = (c % CAP) < cnt[2 * peer + c // CAP]
            row = jnp.where(lane == c, jnp.where(live, pm[slot], -1), row)
        out[peer, PER, 0:1, :] = row.astype(f32)
        return unused

    lax.fori_loop(0, PEERS, one_peer, 0)


def pack(ps, pm, cnt, coords, weight):
    return pl.pallas_call(
        pack_kernel,
        name="pack",
        out_shape=jax.ShapeDtypeStruct((PEERS, PER + 1, 4, QP), f32),
        in_specs=[SMEM_SPEC] * 3 + [VMEM_SPEC] * 2,
        out_specs=VMEM_SPEC,
    )(ps, pm, cnt, coords, weight)


def front(tile, y8, keep):
    wide = jnp.concatenate([tile, tile], axis=0)
    rows = lax.broadcasted_iota(jnp.int32, (8, 128), 0)
    centre = pltpu.roll(y8[:, :128], 3, 0)
    xs = jnp.where(rows < 3, (wide - centre) * SCALE, 0.0)
    norm = -0.5 * jnp.sum(xs * xs, axis=0, keepdims=True)
    weight = wide[3:4]
    x8 = jnp.where(rows == 3, norm, jnp.where(rows == 4, 1.0, xs))
    x1 = narrow(x8)
    x2 = narrow(x8 - x1)
    x3 = x8 - x1 - x2
    y1 = narrow(y8)
    y2 = narrow(y8 - y1)
    y3 = y8 - y1 - y2
    left = jnp.concatenate([x1, x1, x2, x2, x1, x3], axis=0).astype(bf16)
    lead = jnp.concatenate([y1, y2], axis=0).astype(bf16)
    tail = jnp.concatenate([y3, y1], axis=0).astype(bf16)
    right = jnp.concatenate([lead, lead, tail], axis=0)
    gauss = jnp.exp2(dot(left, right, 0, 0))
    high = gauss.astype(bf16)
    low = (gauss - high.astype(f32)).astype(bf16)
    ax = x8 * (weight * keep)
    ax1 = narrow(ax)
    ax = jnp.concatenate([ax1, ax - ax1], axis=0).astype(bf16)
    return high, low, ax, lead, xs, jnp.broadcast_to(weight * GAIN, (8, 128))


PIECES = 6


def force_kernel(meta, core, tiles, y8, force, acc, entries, *buffers):
    acc[...] = jnp.zeros_like(acc)
    mine = core[0]
    entries[0] = 0

    def list_peer(peer, count):
        for c in range(PER):
            block = meta[peer * PER + c]
            half = (c // CAP) ^ mine
            entries[count] = (peer * 16 + c) | ((half * MB + block) << 10)
            count = count + (block >= 0).astype(jnp.int32)
        return count

    total = lax.fori_loop(0, PEERS, list_peer, jnp.int32(0))
    last = entries[jnp.maximum(total - 1, 0)]
    for k in range(3 * GROUP):
        entries[total + k] = last | (1 << 20)
    trips = (total + 2 * GROUP - 1) // (2 * GROUP)

    def unpack(index):
        entry = entries[index]
        return (entry >> 4) & 63, entry & 15, (entry >> 10) & 511, entry >> 20

    def stage_front(group, which):
        for u in range(GROUP):
            peer, c, block, extra = unpack(group * GROUP + u)
            keep = (1 - extra).astype(f32)
            base = (which * GROUP + u) * PIECES
            values = front(tiles[peer, c], y8[block], keep)
            for k in range(PIECES):
                buffers[base + k][...] = values[k]

    def stage_back(group, which):
        for u in range(GROUP):
            peer, c, block, extra = unpack(group * GROUP + u)
            base = (which * GROUP + u) * PIECES
            high, low, ax, lead, xs, scale = [buffers[base + k][...] for k in range(PIECES)]
            q = dot(ax, high, 1, 0) + dot(ax, low, 1, 0)
            f = dot(lead, high, 1, 1) + dot(lead, low, 1, 1)
            f = f[0:8] + f[8:16]
            f = scale * (xs * f[3:4] - f)
            force[peer, pl.ds(c * 3, 3), :] = f[0:3]
            acc[block] = acc[block] + (q[0:8] + q[8:16])

    stage_front(0, 0)

    def trip(i, unused):
        stage_front(2 * i + 1, 1)
        stage_back(2 * i, 0)
        stage_front(2 * i + 2, 0)
        stage_back(2 * i + 1, 1)
        return unused

    lax.fori_loop(0, trips, trip, 0)


def forces(meta, core, tiles, y8):
    one = [
        pltpu.VMEM((QP, MP), bf16),
        pltpu.VMEM((QP, MP), bf16),
        pltpu.VMEM((16, QP), bf16),
        pltpu.VMEM((16, MP), bf16),
        pltpu.VMEM((8, QP), f32),
        pltpu.VMEM((8, QP), f32),
    ]
    return pl.pallas_call(
        force_kernel,
        name="forces",
        out_shape=(
            jax.ShapeDtypeStruct((PEERS, FROWS, QP), f32),
            jax.ShapeDtypeStruct((2 * MB, 8, MP), f32),
        ),
        in_specs=[SMEM_SPEC, SMEM_SPEC, VMEM_SPEC, VMEM_SPEC],
        out_specs=(VMEM_SPEC, VMEM_SPEC),
        scratch_shapes=[pltpu.SMEM((PEERS * PER + 3 * GROUP,), jnp.int32)] + one * (2 * GROUP),
    )(meta, core, tiles, y8)


def gather_kernel(ps, cnt, force, out, even, odd):
    even[...] = jnp.zeros_like(even)
    odd[...] = jnp.zeros_like(odd)

    def one_peer(peer, unused):
        for c in range(PER):
            live = (c % CAP) < cnt[2 * peer + c // CAP]
            block = jnp.where(live, ps[peer * PER + c], SB)
            total = odd if c % 2 else even
            total[block] = total[block] + force[peer, 3 * c : 3 * c + 3, :]
        return unused

    lax.fori_loop(0, PEERS, one_peer, 0)
    out[...] = even[0:SB] + odd[0:SB]


def gather_forces(ps, cnt, force):
    return pl.pallas_call(
        gather_kernel,
        name="gather",
        out_shape=jax.ShapeDtypeStruct((SB, 3, QP), f32),
        in_specs=[SMEM_SPEC] * 2 + [VMEM_SPEC],
        out_specs=VMEM_SPEC,
        scratch_shapes=[pltpu.VMEM((SB + 1, 3, QP), f32)] * 2,
    )(ps, cnt, force)


def exchange(x):
    return lax.all_to_all(x, ("gx", "g"), split_axis=0, concat_axis=0, tiled=True)


def swap(x):
    return lax.ppermute(x, "core", [(0, 1), (1, 0)])


def spread_table():
    return jnp.kron(jnp.eye(16, dtype=f32), bezier_table())


def body(slave_coords, slave_weight, master_ctrl, master_wt, pair_slave, pair_master, pair_count):
    coords = slave_coords.reshape(3, SB, QP).transpose(1, 0, 2)
    payload = pack(
        pair_slave, pair_master, pair_count, coords, slave_weight.reshape(SB, QP)
    )
    tiles = exchange(payload)

    own = jnp.concatenate([master_ctrl, master_wt[None, :]], axis=0).reshape(4, MB, MP)
    both = jnp.concatenate([own, swap(own)], axis=1)
    table = spread_table()
    lifted = jnp.concatenate([both[:3] * both[3:], both[3:]], axis=0)
    summed = jnp.einsum("cbk,jk->cbj", lifted, table, precision=lax.Precision.HIGHEST)
    samples = summed[:3] / summed[3:]
    centre = jnp.mean(samples, axis=2, keepdims=True)
    scaled = (samples - centre) * SCALE
    norm = -0.5 * jnp.sum(scaled * scaled, axis=0, keepdims=True)
    y8 = jnp.concatenate(
        [scaled, jnp.ones_like(norm), norm, jnp.broadcast_to(centre, scaled.shape)], axis=0
    ).transpose(1, 0, 2)

    core = lax.axis_index("core").reshape(1).astype(jnp.int32)
    meta = tiles[:, PER, 0, :PER].astype(jnp.int32).reshape(PEERS * PER)
    force, acc = forces(meta, core, tiles, y8)

    force = exchange(force)
    slave_force = gather_forces(pair_slave, pair_count, force)

    acc = acc.transpose(1, 0, 2)
    q = (scaled * acc[4:5] - acc[0:3]) * GAIN
    q = q[:, :MB] + swap(q[:, MB:])
    master_force = (
        jnp.einsum(
            "cbj,jk->cbk", q / summed[3:, :MB], table, precision=lax.Precision.HIGHEST
        )
        * own[3:]
    )
    return (
        slave_force.transpose(1, 0, 2).reshape(3, SB * QP),
        master_force.reshape(3, MB * MP),
    )


def solution(mesh):
    split = Mesh(mesh.devices.reshape(4, 16, 2), ("gx", "g", "core"))
    every = ("gx", "g", "core")
    wide, flat = P(None, every), P(every)
    return jax.shard_map(
        body,
        mesh=split,
        in_specs=(wide, flat, wide, flat, flat, flat, flat),
        out_specs=(wide, wide),
        check_vma=False,
    )
```

```python
import functools
import math

import jax
import jax.numpy as jnp
from jax import lax
from jax.experimental import pallas as pl
from jax.experimental.pallas import tpu as pltpu
from jax.sharding import Mesh
from jax.sharding import PartitionSpec as P

QP = 128
CAP = 5
SB = 512
MB = 256
MP = 256
PEERS = 64
GROUP = 4

f32 = jnp.float32
bf16 = jnp.bfloat16
fp8 = jnp.float8_e4m3fn
SCALE = math.sqrt(2.0 * math.log2(math.e) / 3.0)
GAIN = 0.01 / SCALE

VMEM_SPEC = pl.BlockSpec(memory_space=pltpu.VMEM)
ANY_SPEC = pl.BlockSpec(memory_space=pl.ANY)
SMEM_SPEC = pl.BlockSpec(memory_space=pltpu.SMEM)


def bezier_table():
    params = (jnp.arange(4, dtype=f32) + 0.5) / 4.0
    powers = jnp.arange(4, dtype=f32)
    binomial = jnp.array([1.0, 3.0, 3.0, 1.0], dtype=f32)
    bernstein = (
        binomial[None, :]
        * params[:, None] ** powers[None, :]
        * (1.0 - params[:, None]) ** (3.0 - powers[None, :])
    )
    return (bernstein[:, None, :, None] * bernstein[None, :, None, :]).reshape(16, 16)


def dot(a, b, left, right):
    return lax.dot_general(a, b, (((left,), (right,)), ((), ())), preferred_element_type=f32)


def narrow(x):
    return x.astype(bf16).astype(f32)


def pack_kernel(low, size, ps, pm, cnt, coords, weight, out):
    lane = lax.broadcasted_iota(jnp.int32, (1, 128), 1)

    def one_peer(peer, unused):
        row = jnp.zeros((1, 128), jnp.int32)
        for half in range(2):
            owner = 2 * peer + half
            for c in range(size):
                slot = owner * CAP + low + c
                block = ps[slot]
                spot = half * size + c
                out[peer, spot, 0:3, :] = coords[block]
                out[peer, spot, 3:4, :] = weight[pl.ds(block, 1), :]
                row = jnp.where(lane == spot, pm[slot], row)
            live = jnp.clip(cnt[owner] - low, 0, size)
            row = jnp.where(lane == 2 * size + half, live, row)
        out[peer, 2 * size, 0:1, :] = row.astype(f32)
        return unused

    lax.fori_loop(0, PEERS, one_peer, 0)


def pack(low, size, ps, pm, cnt, coords, weight):
    return pl.pallas_call(
        functools.partial(pack_kernel, low, size),
        name="pack",
        out_shape=jax.ShapeDtypeStruct((PEERS, 2 * size + 1, 4, QP), f32),
        in_specs=[SMEM_SPEC] * 3 + [VMEM_SPEC] * 2,
        out_specs=VMEM_SPEC,
    )(ps, pm, cnt, coords, weight)


def sample_kernel(own, other, y8):
    def eight(source, base):
        def one(i, unused):
            at = pl.ds(pl.multiple_of(i * 8, 8), 8)
            inverse = 1.0 / source[3, at, :]
            norm = jnp.zeros((8, MP), f32)
            spot = (base + i * 8) * 8
            for k in range(3):
                y = source[k, at, :] * inverse
                centre = jnp.sum(y, axis=1, keepdims=True) * (1.0 / MP)
                y = (y - centre) * SCALE
                norm = norm - 0.5 * (y * y)
                for h in range(2):
                    lanes = slice(128 * h, 128 * h + 128)
                    y8[h, pl.ds(spot + k, 8, stride=8), :] = y[:, lanes]
                    y8[h, pl.ds(spot + 5 + k, 8, stride=8), :] = jnp.broadcast_to(centre, (8, 128))
            for h in range(2):
                lanes = slice(128 * h, 128 * h + 128)
                y8[h, pl.ds(spot + 3, 8, stride=8), :] = jnp.ones((8, 128), f32)
                y8[h, pl.ds(spot + 4, 8, stride=8), :] = norm[:, lanes]
            return unused

        lax.fori_loop(0, MB // 8, one, 0, unroll=2)

    eight(own, 0)
    eight(other, MB)


def sample_tiles(own, other):
    return pl.pallas_call(
        sample_kernel,
        name="samples",
        out_shape=jax.ShapeDtypeStruct((2, 2 * MB * 8, 128), f32),
        in_specs=[VMEM_SPEC] * 2,
        out_specs=VMEM_SPEC,
    )(own, other)


def front(tile, y8, keep):
    wide = jnp.concatenate([tile, tile], axis=0)
    rows = lax.broadcasted_iota(jnp.int32, (8, 128), 0)
    centre = pltpu.roll(y8[:, :128], 3, 0)
    xs = jnp.where(rows < 3, (wide - centre) * SCALE, 0.0)
    norm = -0.5 * jnp.sum(xs * xs, axis=0, keepdims=True)
    weight = wide[3:4]
    x8 = jnp.where(rows == 3, norm, jnp.where(rows == 4, 1.0, xs))
    x1 = narrow(x8)
    x2 = narrow(x8 - x1)
    x3 = x8 - x1 - x2
    y1 = narrow(y8)
    y2 = narrow(y8 - y1)
    y3 = y8 - y1 - y2
    left = jnp.concatenate([x1, x1, x2, x2, x1, x3], axis=0).astype(bf16)
    lead = jnp.concatenate([y1, y2], axis=0).astype(bf16)
    tail = jnp.concatenate([y3, y1], axis=0).astype(bf16)
    right = jnp.concatenate([lead, lead, tail], axis=0)
    gauss = jnp.exp2(dot(left, right, 0, 0))
    high = gauss.astype(bf16)
    low = ((gauss - high.astype(f32)) * LIFT).astype(fp8)
    ax = x8 * (weight * keep)
    ax1 = narrow(ax)
    ax2 = jnp.concatenate([ax1, ax - ax1], axis=0).astype(bf16)
    ax8 = jnp.concatenate([ax] * 4, axis=0).astype(fp8)
    lead8 = jnp.concatenate([y8] * 4, axis=0).astype(fp8)
    return high, low, ax2, ax8, lead, lead8, xs, jnp.broadcast_to(weight * GAIN, (8, 128))


PIECES = 8
LIFT = 65536.0


def force_kernel(size, core, tiles_hbm, y8_hbm, force, own, other, tiles, y8, acc, meta, sems, entries, *buffers):
    load_meta = pltpu.make_async_copy(tiles_hbm.at[:, 2 * size, 0, :], meta, sems.at[0])
    load_tiles = pltpu.make_async_copy(tiles_hbm, tiles, sems.at[1])
    load_y8 = pltpu.make_async_copy(y8_hbm, y8, sems.at[2])
    load_meta.start()
    load_tiles.start()
    load_y8.start()
    acc[...] = jnp.zeros_like(acc)
    mine = core[0]
    load_meta.wait()

    def list_peer(peer, count):
        for half in range(2):
            base = (peer * 16) | (((half ^ mine) * MB) << 10)
            for c in range(size):
                spot = half * size + c
                block = meta[peer, spot].astype(jnp.int32)
                entries[count + c] = (base + spot) | (block << 10)
            count = count + meta[peer, 2 * size + half].astype(jnp.int32)
        return count

    total = lax.fori_loop(0, PEERS, list_peer, jnp.int32(0))
    last = entries[jnp.maximum(total - 1, 0)]
    for k in range(3 * GROUP):
        entries[total + k] = last | (1 << 20)
    trips = (total + 2 * GROUP - 1) // (2 * GROUP)
    load_tiles.wait()
    load_y8.wait()

    def unpack(index):
        entry = entries[index]
        return (entry >> 4) & 63, entry & 15, (entry >> 10) & 511, entry >> 20

    def stage_front(group, which):
        for u in range(GROUP):
            peer, c, block, extra = unpack(group * GROUP + u)
            keep = (1 - extra).astype(f32)
            base = (which * GROUP + u) * PIECES
            at = pl.ds(pl.multiple_of(block * 8, 8), 8)
            samples = jnp.concatenate([y8[0, at, :], y8[1, at, :]], axis=1)
            values = front(tiles[peer, c], samples, keep)
            for k in range(PIECES):
                buffers[base + k][...] = values[k]

    def stage_back(group, which):
        for u in range(GROUP):
            peer, c, block, extra = unpack(group * GROUP + u)
            base = (which * GROUP + u) * PIECES
            high, low, ax2, ax8, lead, lead8, xs, scale = [
                buffers[base + k][...] for k in range(PIECES)
            ]
            q = dot(ax2, high, 1, 0)
            f = dot(lead, high, 1, 1)
            q = q[0:8] + q[8:16] + dot(ax8, low, 1, 0)[0:8] * (1.0 / LIFT)
            f = f[0:8] + f[8:16] + dot(lead8, low, 1, 1)[0:8] * (1.0 / LIFT)
            f = scale * (xs * f[3:4] - f)
            force[peer, pl.ds(c * 3, 3), :] = f[0:3]
            at = pl.ds(pl.multiple_of(block * 8, 8), 8)
            for h in range(2):
                acc[h, at, :] = acc[h, at, :] + q[:, 128 * h : 128 * h + 128]

    stage_front(0, 0)

    def trip(i, unused):
        stage_front(2 * i + 1, 1)
        stage_back(2 * i, 0)
        stage_front(2 * i + 2, 0)
        stage_back(2 * i + 1, 1)
        return unused

    lax.fori_loop(0, trips, trip, 0)

    def finish(out, first):
        def one(i, unused):
            spot = (first + i * 8) * 8
            at = pl.ds(pl.multiple_of(i * 8, 8), 8)
            for h in range(2):
                amount = acc[h, pl.ds(spot + 4, 8, stride=8), :]
                for k in range(3):
                    rows = pl.ds(spot + k, 8, stride=8)
                    out[k, at, 128 * h : 128 * h + 128] = (y8[h, rows, :] * amount - acc[h, rows, :]) * GAIN
            return unused

        lax.fori_loop(0, MB // 8, one, 0, unroll=2)

    finish(own, 0)
    finish(other, MB)


def forces(size, core, tiles, y8):
    one = [
        pltpu.VMEM((QP, MP), bf16),
        pltpu.VMEM((QP, MP), fp8),
        pltpu.VMEM((16, QP), bf16),
        pltpu.VMEM((32, QP), fp8),
        pltpu.VMEM((16, MP), bf16),
        pltpu.VMEM((32, MP), fp8),
        pltpu.VMEM((8, QP), f32),
        pltpu.VMEM((8, QP), f32),
    ]
    part = jax.ShapeDtypeStruct((3, MB, MP), f32)
    return pl.pallas_call(
        functools.partial(force_kernel, size),
        name="forces",
        out_shape=(jax.ShapeDtypeStruct((PEERS, force_rows(size), QP), f32), part, part),
        in_specs=[SMEM_SPEC, ANY_SPEC, ANY_SPEC],
        out_specs=(VMEM_SPEC,) * 3,
        scratch_shapes=[
            pltpu.VMEM(tiles.shape, f32),
            pltpu.VMEM(y8.shape, f32),
            pltpu.VMEM(y8.shape, f32),
            pltpu.SMEM((PEERS, 128), f32),
            pltpu.SemaphoreType.DMA((3,)),
            pltpu.SMEM((2 * PEERS * size + CAP + 3 * GROUP,), jnp.int32),
        ]
        + one * (2 * GROUP),
    )(core, tiles, y8)


def force_rows(size):
    return -(-6 * size // 8) * 8


def gather_kernel(low, size, ps, cnt, force, out, even, odd):
    even[...] = jnp.zeros_like(even)
    odd[...] = jnp.zeros_like(odd)

    def one_peer(peer, unused):
        for half in range(2):
            owner = 2 * peer + half
            live = cnt[owner] - low
            for c in range(size):
                block = jnp.where(c < live, ps[owner * CAP + low + c], SB)
                row = 3 * (half * size + c)
                total = odd if (half * size + c) % 2 else even
                total[block] = total[block] + force[peer, row : row + 3, :]
        return unused

    lax.fori_loop(0, PEERS, one_peer, 0)
    out[...] = even[0:SB] + odd[0:SB]


def gather_forces(low, size, ps, cnt, force):
    return pl.pallas_call(
        functools.partial(gather_kernel, low, size),
        name="gather",
        out_shape=jax.ShapeDtypeStruct((SB, 3, QP), f32),
        in_specs=[SMEM_SPEC] * 2 + [VMEM_SPEC],
        out_specs=VMEM_SPEC,
        scratch_shapes=[pltpu.VMEM((SB + 1, 3, QP), f32)] * 2,
    )(ps, cnt, force)


def exchange(x):
    return lax.all_to_all(x, ("gx", "g"), split_axis=0, concat_axis=0, tiled=True)


def swap(x):
    return lax.ppermute(x, "core", [(0, 1), (1, 0)])


def spread_table():
    return jnp.kron(jnp.eye(16, dtype=f32), bezier_table())


def sums(blocks, table):
    lifted = jnp.concatenate([blocks[:3] * blocks[3:], blocks[3:]], axis=0)
    return jnp.einsum("cbk,jk->cbj", lifted, table, precision=lax.Precision.HIGHEST)


def body(slave_coords, slave_weight, master_ctrl, master_wt, pair_slave, pair_master, pair_count):
    coords = slave_coords.reshape(3, SB, QP).transpose(1, 0, 2)
    payload = pack(
        0, CAP, pair_slave, pair_master, pair_count, coords, slave_weight.reshape(SB, QP)
    )
    tiles = exchange(payload)

    blocks = jnp.concatenate([master_ctrl, master_wt[None, :]], axis=0).reshape(4, MB, MP)
    table = spread_table()
    own = sums(blocks, table)
    y8 = sample_tiles(own, sums(swap(blocks), table))

    core = lax.axis_index("core").reshape(1).astype(jnp.int32)
    force, q, away = forces(CAP, core, tiles, y8)
    slave_force = gather_forces(0, CAP, pair_slave, pair_count, exchange(force))

    q = (q + swap(away)) / own[3:]
    master_force = (
        jnp.einsum("cbj,jk->cbk", q, table, precision=lax.Precision.HIGHEST) * blocks[3:]
    )
    return (
        slave_force.transpose(1, 0, 2).reshape(3, SB * QP),
        master_force.reshape(3, MB * MP),
    )


def solution(mesh):
    split = Mesh(mesh.devices.reshape(4, 16, 2), ("gx", "g", "core"))
    every = ("gx", "g", "core")
    wide, flat = P(None, every), P(every)
    return jax.shard_map(
        body,
        mesh=split,
        in_specs=(wide, flat, wide, flat, flat, flat, flat),
        out_specs=(wide, wide),
        check_vma=False,
    )
```

```python
import functools
import math

import jax
import jax.numpy as jnp
import numpy as np
from jax import lax
from jax.experimental import pallas as pl
from jax.experimental.pallas import tpu as pltpu
from jax.sharding import Mesh
from jax.sharding import PartitionSpec as P


QP = 128
CAP = 5
SB = 512
MB = 256
MP = 256
PEERS = 64
GROUP = 8

f32 = jnp.float32
bf16 = jnp.bfloat16
fp8 = jnp.float8_e4m3fn
SCALE = math.sqrt(2.0 * math.log2(math.e) / 3.0)
GAIN = 0.01 / SCALE

VMEM_SPEC = pl.BlockSpec(memory_space=pltpu.VMEM)
ANY_SPEC = pl.BlockSpec(memory_space=pl.ANY)
SMEM_SPEC = pl.BlockSpec(memory_space=pltpu.SMEM)


def bezier_table():
    params = (np.arange(4) + 0.5) / 4.0
    powers = np.arange(4)
    binomial = np.array([1.0, 3.0, 3.0, 1.0])
    bernstein = (
        binomial[None, :]
        * params[:, None] ** powers[None, :]
        * (1.0 - params[:, None]) ** (3.0 - powers[None, :])
    )
    return (bernstein[:, None, :, None] * bernstein[None, :, None, :]).reshape(16, 16)


def spread_table():
    return jnp.asarray(np.kron(np.eye(16), bezier_table()).astype(np.float32))


def dot(a, b, left, right):
    return lax.dot_general(a, b, (((left,), (right,)), ((), ())), preferred_element_type=f32)


def narrow(x):
    return x.astype(bf16).astype(f32)


def pack_kernel(low, size, ps, pm, cnt, coords, weight, out):
    lane = lax.broadcasted_iota(jnp.int32, (1, 128), 1)

    def one_peer(peer, unused):
        row = jnp.zeros((1, 128), jnp.int32)
        for half in range(2):
            owner = 2 * peer + half
            for c in range(size):
                slot = owner * CAP + low + c
                block = ps[slot]
                spot = half * size + c
                out[peer, spot, 0:3, :] = coords[block]
                out[peer, spot, 3:4, :] = weight[pl.ds(block, 1), :]
                row = jnp.where(lane == spot, pm[slot], row)
            live = jnp.clip(cnt[owner] - low, 0, size)
            row = jnp.where(lane == 2 * size + half, live, row)
        out[peer, 2 * size, 0:1, :] = row.astype(f32)
        return unused

    lax.fori_loop(0, PEERS, one_peer, 0)


def pack(low, size, ps, pm, cnt, coords, weight):
    return pl.pallas_call(
        functools.partial(pack_kernel, low, size),
        name="pack",
        out_shape=jax.ShapeDtypeStruct((PEERS, 2 * size + 1, 4, QP), f32),
        in_specs=[SMEM_SPEC] * 3 + [VMEM_SPEC] * 2,
        out_specs=VMEM_SPEC,
    )(ps, pm, cnt, coords, weight)


def sample_kernel(own, other, table, y8, total, sums):
    def halves(source, base):
        def lift(k, unused):
            rows = source[k] * jnp.where(k == 3, 1.0, source[3])
            sums[k] = lax.dot_general(
                rows,
                table[...],
                (((1,), (1,)), ((), ())),
                precision=lax.Precision.HIGHEST,
                preferred_element_type=f32,
            )
            return unused

        lax.fori_loop(0, 4, lift, 0)
        if base == 0:
            total[...] = sums[3]

        def one(i, unused):
            at = pl.ds(pl.multiple_of(i * 8, 8), 8)
            inverse = 1.0 / sums[3, at, :]
            norm = jnp.zeros((8, MP), f32)
            spot = (base + i * 8) * 8
            for k in range(3):
                y = sums[k, at, :] * inverse
                centre = jnp.sum(y, axis=1, keepdims=True) * (1.0 / MP)
                y = (y - centre) * SCALE
                norm = norm - 0.5 * (y * y)
                for h in range(2):
                    lanes = slice(128 * h, 128 * h + 128)
                    y8[h, pl.ds(spot + k, 8, stride=8), :] = y[:, lanes]
                    y8[h, pl.ds(spot + 5 + k, 8, stride=8), :] = jnp.broadcast_to(centre, (8, 128))
            for h in range(2):
                lanes = slice(128 * h, 128 * h + 128)
                y8[h, pl.ds(spot + 3, 8, stride=8), :] = jnp.ones((8, 128), f32)
                y8[h, pl.ds(spot + 4, 8, stride=8), :] = norm[:, lanes]
            return unused

        lax.fori_loop(0, MB // 8, one, 0, unroll=4)

    halves(own, 0)
    halves(other, MB)


def sample_tiles(own, other, table):
    return pl.pallas_call(
        sample_kernel,
        name="samples",
        out_shape=(
            jax.ShapeDtypeStruct((2, 2 * MB * 8, 128), f32),
            jax.ShapeDtypeStruct((MB, MP), f32),
        ),
        in_specs=[VMEM_SPEC] * 3,
        out_specs=(VMEM_SPEC,) * 2,
        scratch_shapes=[pltpu.VMEM((4, MB, MP), f32)],
    )(own, other, table)


def front(tile, y8, keep):
    wide = jnp.concatenate([tile, tile], axis=0)
    rows = lax.broadcasted_iota(jnp.int32, (8, 128), 0)
    centre = pltpu.roll(y8[:, :128], 3, 0)
    xs = jnp.where(rows < 3, (wide - centre) * SCALE, 0.0)
    norm = -0.5 * jnp.sum(xs * xs, axis=0, keepdims=True)
    weight = wide[3:4]
    x8 = jnp.where(rows == 3, norm, jnp.where(rows == 4, 1.0, xs))
    x1 = narrow(x8)
    x2 = narrow(x8 - x1)
    x3 = x8 - x1 - x2
    y1 = narrow(y8)
    y2 = narrow(y8 - y1)
    y3 = y8 - y1 - y2
    left = jnp.concatenate([x1, x1, x2, x2, x1, x3], axis=0).astype(bf16)
    lead = jnp.concatenate([y1, y2], axis=0).astype(bf16)
    tail = jnp.concatenate([y3, y1], axis=0).astype(bf16)
    right = jnp.concatenate([lead, lead, tail], axis=0)
    gauss = jnp.exp2(dot(left, right, 0, 0))
    high = gauss.astype(bf16)
    low = ((gauss - high.astype(f32)) * LIFT).astype(fp8)
    ax = x8 * (weight * keep)
    ax1 = narrow(ax)
    ax2 = jnp.concatenate([ax1, ax - ax1], axis=0).astype(bf16)
    ax8 = jnp.concatenate([ax] * 4, axis=0).astype(fp8)
    lead8 = jnp.concatenate([y8] * 4, axis=0).astype(fp8)
    return high, low, ax2, ax8, lead, lead8, xs, jnp.broadcast_to(weight * GAIN, (8, 128))


PIECES = 8
LIFT = 65536.0


def force_kernel(size, core, tiles, y8_hbm, force, own, other, y8, acc, meta, sems, entries, *buffers):
    load_meta = pltpu.make_async_copy(tiles.at[:, 2 * size, 0, :], meta, sems.at[0])
    load_meta.start()
    load_y8 = pltpu.make_async_copy(y8_hbm, y8, sems.at[1])
    load_y8.start()
    acc[...] = jnp.zeros_like(acc)
    mine = core[0]
    load_meta.wait()

    def list_peer(peer, count):
        for half in range(2):
            base = (peer * 16) | (((half ^ mine) * MB) << 10)
            for c in range(size):
                spot = half * size + c
                block = meta[peer, spot].astype(jnp.int32)
                entries[count + c] = (base + spot) | (block << 10)
            count = count + meta[peer, 2 * size + half].astype(jnp.int32)
        return count

    total = lax.fori_loop(0, PEERS, list_peer, jnp.int32(0))
    last = entries[jnp.maximum(total - 1, 0)]
    for k in range(3 * GROUP):
        entries[total + k] = last | (1 << 20)
    trips = (total + 2 * GROUP - 1) // (2 * GROUP)

    load_y8.wait()

    def unpack(index):
        entry = entries[index]
        return (entry >> 4) & 63, entry & 15, (entry >> 10) & 511, entry >> 20

    def stage_front(group, which):
        for u in range(GROUP):
            peer, c, block, extra = unpack(group * GROUP + u)
            keep = (1 - extra).astype(f32)
            base = (which * GROUP + u) * PIECES
            at = pl.ds(pl.multiple_of(block * 8, 8), 8)
            samples = jnp.concatenate([y8[0, at, :], y8[1, at, :]], axis=1)
            values = front(tiles[peer, c], samples, keep)
            for k in range(PIECES):
                buffers[base + k][...] = values[k]

    def stage_back(group, which):
        for u in range(GROUP):
            peer, c, block, _ = unpack(group * GROUP + u)
            base = (which * GROUP + u) * PIECES
            high, low, ax2, ax8, lead, lead8, xs, scale = [
                buffers[base + k][...] for k in range(PIECES)
            ]
            q = dot(ax2, high, 1, 0)
            f = dot(lead, high, 1, 1)
            q = q[0:8] + q[8:16] + dot(ax8, low, 1, 0)[0:8] * (1.0 / LIFT)
            f = f[0:8] + f[8:16] + dot(lead8, low, 1, 1)[0:8] * (1.0 / LIFT)
            f = scale * (xs * f[3:4] - f)
            force[peer, pl.ds(c * 3, 3), :] = f[0:3]
            at = pl.ds(pl.multiple_of(block * 8, 8), 8)
            for h in range(2):
                acc[h, at, :] = acc[h, at, :] + q[:, 128 * h : 128 * h + 128]

    stage_front(0, 0)

    def trip(i, unused):
        stage_front(2 * i + 1, 1)
        stage_back(2 * i, 0)
        stage_front(2 * i + 2, 0)
        stage_back(2 * i + 1, 1)
        return unused

    lax.fori_loop(0, trips, trip, 0)

    def finish(out, first):
        def one(i, unused):
            spot = (first + i * 8) * 8
            at = pl.ds(pl.multiple_of(i * 8, 8), 8)
            for h in range(2):
                amount = acc[h, pl.ds(spot + 4, 8, stride=8), :]
                for k in range(3):
                    rows = pl.ds(spot + k, 8, stride=8)
                    out[k, at, 128 * h : 128 * h + 128] = (y8[h, rows, :] * amount - acc[h, rows, :]) * GAIN
            return unused

        lax.fori_loop(0, MB // 8, one, 0, unroll=4)

    finish(own, 0)
    finish(other, MB)


def forces(size, core, tiles, y8):
    one = [
        pltpu.VMEM((QP, MP), bf16),
        pltpu.VMEM((QP, MP), fp8),
        pltpu.VMEM((16, QP), bf16),
        pltpu.VMEM((32, QP), fp8),
        pltpu.VMEM((16, MP), bf16),
        pltpu.VMEM((32, MP), fp8),
        pltpu.VMEM((8, QP), f32),
        pltpu.VMEM((8, QP), f32),
    ]
    part = jax.ShapeDtypeStruct((3, MB, MP), f32)
    return pl.pallas_call(
        functools.partial(force_kernel, size),
        name="forces",
        out_shape=(jax.ShapeDtypeStruct((PEERS, force_rows(size), QP), f32), part, part),
        in_specs=[SMEM_SPEC, VMEM_SPEC, ANY_SPEC],
        out_specs=(VMEM_SPEC,) * 3,
        scratch_shapes=[
            pltpu.VMEM(y8.shape, f32),
            pltpu.VMEM(y8.shape, f32),
            pltpu.SMEM((PEERS, 128), f32),
            pltpu.SemaphoreType.DMA((2,)),
            pltpu.SMEM((2 * PEERS * size + CAP + 3 * GROUP,), jnp.int32),
        ]
        + one * (2 * GROUP),
    )(core, tiles, y8)


def force_rows(size):
    return -(-6 * size // 8) * 8


def gather_kernel(low, size, ps, cnt, force, out, even, odd):
    even[...] = jnp.zeros_like(even)
    odd[...] = jnp.zeros_like(odd)

    def one_peer(peer, unused):
        for half in range(2):
            owner = 2 * peer + half
            live = cnt[owner] - low
            for c in range(size):
                block = jnp.where(c < live, ps[owner * CAP + low + c], SB)
                row = 3 * (half * size + c)
                total = odd if (half * size + c) % 2 else even
                total[block] = total[block] + force[peer, row : row + 3, :]
        return unused

    lax.fori_loop(0, PEERS, one_peer, 0)
    out[...] = even[0:SB] + odd[0:SB]


def gather_forces(low, size, ps, cnt, force):
    return pl.pallas_call(
        functools.partial(gather_kernel, low, size),
        name="gather",
        out_shape=jax.ShapeDtypeStruct((SB, 3, QP), f32),
        in_specs=[SMEM_SPEC] * 2 + [VMEM_SPEC],
        out_specs=VMEM_SPEC,
        scratch_shapes=[pltpu.VMEM((SB + 1, 3, QP), f32)] * 2,
    )(ps, cnt, force)


def exchange(x):
    return lax.all_to_all(x, ("gx", "g"), split_axis=0, concat_axis=0, tiled=True)


def swap(x):
    return lax.ppermute(x, "core", [(0, 1), (1, 0)])


def body(slave_coords, slave_weight, master_ctrl, master_wt, pair_slave, pair_master, pair_count):
    coords = slave_coords.reshape(3, SB, QP).transpose(1, 0, 2)
    payload = pack(
        0, CAP, pair_slave, pair_master, pair_count, coords, slave_weight.reshape(SB, QP)
    )
    tiles = exchange(payload)

    blocks = jnp.concatenate([master_ctrl, master_wt[None, :]], axis=0).reshape(4, MB, MP)
    table = spread_table()
    y8, total = sample_tiles(blocks, swap(blocks), table)

    core = lax.axis_index("core").reshape(1).astype(jnp.int32)
    tiles = pltpu.with_memory_space_constraint(tiles, pltpu.VMEM)
    force, q, away = forces(CAP, core, tiles, y8)
    force = exchange(force)
    away = swap(away)
    slave_force = gather_forces(
        0, CAP, pair_slave, pair_count, pltpu.with_memory_space_constraint(force, pltpu.VMEM)
    )

    q = (q + away) / total
    master_force = (
        jnp.einsum("cbj,jk->cbk", q, table, precision=lax.Precision.HIGHEST) * blocks[3:]
    )
    return (
        slave_force.transpose(1, 0, 2).reshape(3, SB * QP),
        master_force.reshape(3, MB * MP),
    )


def solution(mesh):
    split = Mesh(mesh.devices.reshape(4, 16, 2), ("gx", "g", "core"))
    every = ("gx", "g", "core")
    wide, flat = P(None, every), P(every)
    return jax.shard_map(
        body,
        mesh=split,
        in_specs=(wide, flat, wide, flat, flat, flat, flat),
        out_specs=(wide, wide),
        check_vma=False,
    )
```

```python
import functools
import math

import jax
import jax.numpy as jnp
import numpy as np
from jax import lax
from jax.experimental import pallas as pl
from jax.experimental.pallas import tpu as pltpu
from jax.sharding import Mesh
from jax.sharding import PartitionSpec as P


QP = 128
CAP = 5
SB = 512
MB = 256
MP = 256
PEERS = 64
GROUP = 8

f32 = jnp.float32
bf16 = jnp.bfloat16
fp8 = jnp.float8_e4m3fn
SCALE = math.sqrt(2.0 * math.log2(math.e) / 3.0)
GAIN = 0.01 / SCALE

VMEM_SPEC = pl.BlockSpec(memory_space=pltpu.VMEM)
ANY_SPEC = pl.BlockSpec(memory_space=pl.ANY)
SMEM_SPEC = pl.BlockSpec(memory_space=pltpu.SMEM)


def bezier_table():
    params = (np.arange(4) + 0.5) / 4.0
    powers = np.arange(4)
    binomial = np.array([1.0, 3.0, 3.0, 1.0])
    bernstein = (
        binomial[None, :]
        * params[:, None] ** powers[None, :]
        * (1.0 - params[:, None]) ** (3.0 - powers[None, :])
    )
    return (bernstein[:, None, :, None] * bernstein[None, :, None, :]).reshape(16, 16)


def spread_table():
    return jnp.asarray(np.kron(np.eye(16), bezier_table()).astype(np.float32))


def dot(a, b, left, right):
    return lax.dot_general(a, b, (((left,), (right,)), ((), ())), preferred_element_type=f32)


def narrow(x):
    return x.astype(bf16).astype(f32)


def pack_kernel(size, ps, pm, cnt, coords, weight, out, built, sems):
    lane = lax.broadcasted_iota(jnp.int32, (1, 128), 1)
    share = PEERS // PARTS

    def one_peer(peer, unused):
        row = jnp.zeros((1, 128), jnp.int32)
        for spot in range(2 * size):
            slot = peer * (2 * size) + spot
            block = ps[slot]
            built[peer, spot, 0:3, :] = coords[block]
            built[peer, spot, 3:4, :] = weight[pl.ds(block, 1), :]
            row = jnp.where(lane == spot, pm[slot], row)
        for owner in range(2):
            row = jnp.where(lane == 2 * size + owner, cnt[2 * peer + owner], row)
        built[peer, 2 * size, 0:1, :] = row.astype(f32)
        return unused

    copies = []
    for part in range(PARTS):
        lax.fori_loop(part * share, (part + 1) * share, one_peer, 0, unroll=2)
        some = pl.ds(part * share, share)
        copies.append(pltpu.make_async_copy(built.at[some], out.at[some], sems.at[part]))
        copies[-1].start()
    for copy in copies:
        copy.wait()


PARTS = 4


def pack(size, ps, pm, cnt, coords, weight):
    shape = (PEERS, 2 * size + 1, 4, QP)
    return pl.pallas_call(
        functools.partial(pack_kernel, size),
        name="pack",
        out_shape=jax.ShapeDtypeStruct(shape, f32),
        in_specs=[SMEM_SPEC] * 3 + [VMEM_SPEC] * 2,
        out_specs=ANY_SPEC,
        scratch_shapes=[pltpu.VMEM(shape, f32), pltpu.SemaphoreType.DMA((PARTS,))],
    )(ps, pm, cnt, coords, weight)


def sample_kernel(own, other, table, y8, total, sums):
    def halves(source, base):
        def lift(k, unused):
            rows = source[k] * jnp.where(k == 3, 1.0, source[3])
            sums[k] = lax.dot_general(
                rows,
                table[...],
                (((1,), (1,)), ((), ())),
                precision=lax.Precision.HIGHEST,
                preferred_element_type=f32,
            )
            return unused

        lax.fori_loop(0, 4, lift, 0)
        if base == 0:
            total[...] = sums[3]

        def one(i, unused):
            at = pl.ds(pl.multiple_of(i * 8, 8), 8)
            inverse = 1.0 / sums[3, at, :]
            norm = jnp.zeros((8, MP), f32)
            spot = (base + i * 8) * 8
            for k in range(3):
                y = sums[k, at, :] * inverse
                centre = jnp.sum(y, axis=1, keepdims=True) * (1.0 / MP)
                y = (y - centre) * SCALE
                norm = norm - 0.5 * (y * y)
                for h in range(2):
                    lanes = slice(128 * h, 128 * h + 128)
                    y8[h, pl.ds(spot + k, 8, stride=8), :] = y[:, lanes]
                    y8[h, pl.ds(spot + 5 + k, 8, stride=8), :] = jnp.broadcast_to(centre, (8, 128))
            for h in range(2):
                lanes = slice(128 * h, 128 * h + 128)
                y8[h, pl.ds(spot + 3, 8, stride=8), :] = jnp.ones((8, 128), f32)
                y8[h, pl.ds(spot + 4, 8, stride=8), :] = norm[:, lanes]
            return unused

        lax.fori_loop(0, MB // 8, one, 0, unroll=4)

    halves(own, 0)
    halves(other, MB)


def sample_tiles(own, other, table):
    return pl.pallas_call(
        sample_kernel,
        name="samples",
        out_shape=(
            jax.ShapeDtypeStruct((2, 2 * MB * 8, 128), f32),
            jax.ShapeDtypeStruct((MB, MP), f32),
        ),
        in_specs=[VMEM_SPEC] * 3,
        out_specs=(VMEM_SPEC,) * 2,
        scratch_shapes=[pltpu.VMEM((4, MB, MP), f32)],
    )(own, other, table)


def front(tile, y8, keep):
    wide = jnp.concatenate([tile, tile], axis=0)
    rows = lax.broadcasted_iota(jnp.int32, (8, 128), 0)
    centre = pltpu.roll(y8[:, :128], 3, 0)
    xs = jnp.where(rows < 3, (wide - centre) * SCALE, 0.0)
    norm = -0.5 * jnp.sum(xs * xs, axis=0, keepdims=True)
    weight = wide[3:4]
    x8 = jnp.where(rows == 3, norm, jnp.where(rows == 4, 1.0, xs))
    x1 = narrow(x8)
    x2 = narrow(x8 - x1)
    x3 = x8 - x1 - x2
    y1 = narrow(y8)
    y2 = narrow(y8 - y1)
    y3 = y8 - y1 - y2
    left = jnp.concatenate([x1, x1, x2, x2, x1, x3], axis=0).astype(bf16)
    lead = jnp.concatenate([y1, y2], axis=0).astype(bf16)
    tail = jnp.concatenate([y3, y1], axis=0).astype(bf16)
    right = jnp.concatenate([lead, lead, tail], axis=0)
    gauss = jnp.exp2(dot(left, right, 0, 0))
    high = gauss.astype(bf16)
    low = ((gauss - high.astype(f32)) * LIFT).astype(fp8)
    ax = x8 * (weight * keep)
    ax1 = narrow(ax)
    ax2 = jnp.concatenate([ax1, ax - ax1], axis=0).astype(bf16)
    ax8 = jnp.concatenate([ax] * 4, axis=0).astype(fp8)
    lead8 = jnp.concatenate([y8] * 4, axis=0).astype(fp8)
    return high, low, ax2, ax8, lead, lead8, xs, jnp.broadcast_to(weight * GAIN, (8, 128))


PIECES = 8
LIFT = 65536.0


def force_kernel(size, core, tiles, y8_hbm, force, own, other, y8, acc, rows, meta, sems, entries, *buffers):
    load_y8 = pltpu.make_async_copy(y8_hbm, y8, sems.at[1])
    load_y8.start()

    def row_of(peer, unused):
        rows[pl.ds(peer, 1), :] = tiles[peer, 2 * size, 0:1, :].astype(jnp.int32)
        return unused

    lax.fori_loop(0, PEERS, row_of, 0, unroll=8)
    lane = lax.broadcasted_iota(jnp.int32, (PEERS, 128), 1)
    chip = lax.broadcasted_iota(jnp.int32, (PEERS, 128), 0)
    mine = core[0]
    half = jnp.where(lane < size, mine, 1 - mine)
    sent = rows[...]
    rows[...] = jnp.where(
        lane < 2 * size, (half * MB + sent) * 1024 + chip * 16 + lane, sent
    )
    load_meta = pltpu.make_async_copy(rows, meta, sems.at[0])
    load_meta.start()
    acc[...] = jnp.zeros_like(acc)
    load_meta.wait()

    def list_peer(peer, count):
        for half in range(2):
            for c in range(size):
                entries[count + c] = meta[peer, half * size + c]
            count = count + meta[peer, 2 * size + half]
        return count

    total = lax.fori_loop(0, PEERS, list_peer, jnp.int32(0), unroll=2)
    last = entries[jnp.maximum(total - 1, 0)]
    for k in range(3 * GROUP):
        entries[total + k] = last | (1 << 20)
    trips = (total + 2 * GROUP - 1) // (2 * GROUP)

    load_y8.wait()

    def unpack(index):
        entry = entries[index]
        return (entry >> 4) & 63, entry & 15, (entry >> 10) & 511, entry >> 20

    def stage_front(group, which):
        for u in range(GROUP):
            peer, c, block, extra = unpack(group * GROUP + u)
            keep = (1 - extra).astype(f32)
            base = (which * GROUP + u) * PIECES
            at = pl.ds(pl.multiple_of(block * 8, 8), 8)
            samples = jnp.concatenate([y8[0, at, :], y8[1, at, :]], axis=1)
            values = front(tiles[peer, c], samples, keep)
            for k in range(PIECES):
                buffers[base + k][...] = values[k]

    def stage_back(group, which):
        for u in range(GROUP):
            peer, c, block, _ = unpack(group * GROUP + u)
            base = (which * GROUP + u) * PIECES
            high, low, ax2, ax8, lead, lead8, xs, scale = [
                buffers[base + k][...] for k in range(PIECES)
            ]
            q = dot(ax2, high, 1, 0)
            f = dot(lead, high, 1, 1)
            q = q[0:8] + q[8:16] + dot(ax8, low, 1, 0)[0:8] * (1.0 / LIFT)
            f = f[0:8] + f[8:16] + dot(lead8, low, 1, 1)[0:8] * (1.0 / LIFT)
            f = scale * (xs * f[3:4] - f)
            force[peer, pl.ds(c * 3, 3), :] = f[0:3]
            at = pl.ds(pl.multiple_of(block * 8, 8), 8)
            for h in range(2):
                acc[h, at, :] = acc[h, at, :] + q[:, 128 * h : 128 * h + 128]

    stage_front(0, 0)

    def trip(i, unused):
        stage_front(2 * i + 1, 1)
        stage_back(2 * i, 0)
        stage_front(2 * i + 2, 0)
        stage_back(2 * i + 1, 1)
        return unused

    lax.fori_loop(0, trips, trip, 0)

    def finish(out, first):
        def one(i, unused):
            spot = (first + i * 8) * 8
            at = pl.ds(pl.multiple_of(i * 8, 8), 8)
            for h in range(2):
                amount = acc[h, pl.ds(spot + 4, 8, stride=8), :]
                for k in range(3):
                    rows = pl.ds(spot + k, 8, stride=8)
                    out[k, at, 128 * h : 128 * h + 128] = (y8[h, rows, :] * amount - acc[h, rows, :]) * GAIN
            return unused

        lax.fori_loop(0, MB // 8, one, 0, unroll=4)

    finish(own, 0)
    finish(other, MB)


def forces(size, core, tiles, y8):
    one = [
        pltpu.VMEM((QP, MP), bf16),
        pltpu.VMEM((QP, MP), fp8),
        pltpu.VMEM((16, QP), bf16),
        pltpu.VMEM((32, QP), fp8),
        pltpu.VMEM((16, MP), bf16),
        pltpu.VMEM((32, MP), fp8),
        pltpu.VMEM((8, QP), f32),
        pltpu.VMEM((8, QP), f32),
    ]
    part = jax.ShapeDtypeStruct((3, MB, MP), f32)
    return pl.pallas_call(
        functools.partial(force_kernel, size),
        name="forces",
        out_shape=(jax.ShapeDtypeStruct((PEERS, force_rows(size), QP), f32), part, part),
        in_specs=[SMEM_SPEC, VMEM_SPEC, ANY_SPEC],
        out_specs=(VMEM_SPEC,) * 3,
        scratch_shapes=[
            pltpu.VMEM(y8.shape, f32),
            pltpu.VMEM(y8.shape, f32),
            pltpu.VMEM((PEERS, 128), jnp.int32),
            pltpu.SMEM((PEERS, 128), jnp.int32),
            pltpu.SemaphoreType.DMA((2,)),
            pltpu.SMEM((2 * PEERS * size + CAP + 3 * GROUP,), jnp.int32),
        ]
        + one * (2 * GROUP),
    )(core, tiles, y8)


def force_rows(size):
    return -(-6 * size // 8) * 8


def gather_kernel(low, size, ps, cnt, force, out, even, odd):
    even[...] = jnp.zeros_like(even)
    odd[...] = jnp.zeros_like(odd)

    def one_peer(peer, unused):
        for half in range(2):
            owner = 2 * peer + half
            live = cnt[owner] - low
            for c in range(size):
                block = jnp.where(c < live, ps[peer * (2 * CAP) + half * CAP + low + c], SB)
                row = 3 * (half * size + c)
                total = odd if (half * size + c) % 2 else even
                total[block] = total[block] + force[peer, row : row + 3, :]
        return unused

    lax.fori_loop(0, PEERS, one_peer, 0, unroll=2)
    out[...] = even[0:SB] + odd[0:SB]


def gather_forces(low, size, ps, cnt, force):
    return pl.pallas_call(
        functools.partial(gather_kernel, low, size),
        name="gather",
        out_shape=jax.ShapeDtypeStruct((SB, 3, QP), f32),
        in_specs=[SMEM_SPEC] * 2 + [VMEM_SPEC],
        out_specs=VMEM_SPEC,
        scratch_shapes=[pltpu.VMEM((SB + 1, 3, QP), f32)] * 2,
    )(ps, cnt, force)


def exchange(x):
    return lax.all_to_all(x, ("gx", "g"), split_axis=0, concat_axis=0, tiled=True)


def swap(x):
    return lax.ppermute(x, "core", [(0, 1), (1, 0)])


def body(slave_coords, slave_weight, master_ctrl, master_wt, pair_slave, pair_master, pair_count):
    coords = slave_coords.reshape(3, SB, QP).transpose(1, 0, 2)
    payload = pack(
        CAP, pair_slave, pair_master, pair_count, coords, slave_weight.reshape(SB, QP)
    )
    tiles = exchange(payload)

    blocks = jnp.concatenate([master_ctrl, master_wt[None, :]], axis=0).reshape(4, MB, MP)
    table = spread_table()
    y8, total = sample_tiles(blocks, swap(blocks), table)

    core = lax.axis_index("core").reshape(1).astype(jnp.int32)
    tiles = pltpu.with_memory_space_constraint(tiles, pltpu.VMEM)
    force, q, away = forces(CAP, core, tiles, y8)
    force = exchange(force)
    away = swap(away)
    slave_force = gather_forces(
        0, CAP, pair_slave, pair_count, pltpu.with_memory_space_constraint(force, pltpu.VMEM)
    )

    q = (q + away) / total
    master_force = (
        jnp.einsum("cbj,jk->cbk", q, table, precision=lax.Precision.HIGHEST) * blocks[3:]
    )
    return (
        slave_force.transpose(1, 0, 2).reshape(3, SB * QP),
        master_force.reshape(3, MB * MP),
    )


def solution(mesh):
    split = Mesh(mesh.devices.reshape(4, 16, 2), ("gx", "g", "core"))
    every = ("gx", "g", "core")
    wide, flat = P(None, every), P(every)
    return jax.shard_map(
        body,
        mesh=split,
        in_specs=(wide, flat, wide, flat, flat, flat, flat),
        out_specs=(wide, wide),
        check_vma=False,
    )
```

```python
import functools
import math

import jax
import jax.numpy as jnp
import numpy as np
from jax import lax
from jax.experimental import pallas as pl
from jax.experimental.pallas import tpu as pltpu
from jax.sharding import Mesh
from jax.sharding import PartitionSpec as P


QP = 128
CAP = 5
SB = 512
MB = 256
MP = 256
PEERS = 64
TRIP = 32
LAG = 4
RING = 8
SPARE = TRIP + LAG

f32 = jnp.float32
bf16 = jnp.bfloat16
fp8 = jnp.float8_e4m3fn
SCALE = math.sqrt(2.0 * math.log2(math.e) / 3.0)
GAIN = 0.01 / SCALE

VMEM_SPEC = pl.BlockSpec(memory_space=pltpu.VMEM)
ANY_SPEC = pl.BlockSpec(memory_space=pl.ANY)
SMEM_SPEC = pl.BlockSpec(memory_space=pltpu.SMEM)


def bezier_table():
    params = (np.arange(4) + 0.5) / 4.0
    powers = np.arange(4)
    binomial = np.array([1.0, 3.0, 3.0, 1.0])
    bernstein = (
        binomial[None, :]
        * params[:, None] ** powers[None, :]
        * (1.0 - params[:, None]) ** (3.0 - powers[None, :])
    )
    return (bernstein[:, None, :, None] * bernstein[None, :, None, :]).reshape(16, 16)


def spread_table():
    return jnp.asarray(np.kron(np.eye(16), bezier_table()).astype(np.float32))


def dot(a, b, left, right):
    return lax.dot_general(a, b, (((left,), (right,)), ((), ())), preferred_element_type=f32)


def narrow(x):
    return x.astype(bf16).astype(f32)


def pack_kernel(size, ps, pm, cnt, coords, weight, out, built, sems):
    lane = lax.broadcasted_iota(jnp.int32, (1, 128), 1)
    share = PEERS // PARTS

    def one_peer(peer, unused):
        row = jnp.zeros((1, 128), jnp.int32)
        for spot in range(2 * size):
            slot = peer * (2 * size) + spot
            block = ps[slot]
            built[peer, spot, 0:3, :] = coords[block]
            built[peer, spot, 3:4, :] = weight[pl.ds(block, 1), :]
            row = jnp.where(lane == spot, pm[slot], row)
        for owner in range(2):
            row = jnp.where(lane == 2 * size + owner, cnt[2 * peer + owner], row)
        built[peer, 2 * size, 0:1, :] = row.astype(f32)
        return unused

    copies = []
    for part in range(PARTS):
        lax.fori_loop(part * share, (part + 1) * share, one_peer, 0, unroll=2)
        some = pl.ds(part * share, share)
        copies.append(pltpu.make_async_copy(built.at[some], out.at[some], sems.at[part]))
        copies[-1].start()
    for copy in copies:
        copy.wait()


PARTS = 4


def pack(size, ps, pm, cnt, coords, weight):
    shape = (PEERS, 2 * size + 1, 4, QP)
    return pl.pallas_call(
        functools.partial(pack_kernel, size),
        name="pack",
        out_shape=jax.ShapeDtypeStruct(shape, f32),
        in_specs=[SMEM_SPEC] * 3 + [VMEM_SPEC] * 2,
        out_specs=ANY_SPEC,
        scratch_shapes=[pltpu.VMEM(shape, f32), pltpu.SemaphoreType.DMA((PARTS,))],
    )(ps, pm, cnt, coords, weight)


def sample_kernel(own, other, table, y8, total, sums):
    def halves(source, base):
        def lift(k, unused):
            rows = source[k] * jnp.where(k == 3, 1.0, source[3])
            sums[k] = lax.dot_general(
                rows,
                table[...],
                (((1,), (1,)), ((), ())),
                precision=lax.Precision.HIGHEST,
                preferred_element_type=f32,
            )
            return unused

        lax.fori_loop(0, 4, lift, 0)
        if base == 0:
            total[...] = sums[3]

        def one(i, unused):
            at = pl.ds(pl.multiple_of(i * 8, 8), 8)
            inverse = 1.0 / sums[3, at, :]
            norm = jnp.zeros((8, MP), f32)
            spot = (base + i * 8) * 8
            for k in range(3):
                y = sums[k, at, :] * inverse
                centre = jnp.sum(y, axis=1, keepdims=True) * (1.0 / MP)
                y = (y - centre) * SCALE
                norm = norm - 0.5 * (y * y)
                for h in range(2):
                    lanes = slice(128 * h, 128 * h + 128)
                    y8[h, pl.ds(spot + k, 8, stride=8), :] = y[:, lanes]
                    y8[h, pl.ds(spot + 5 + k, 8, stride=8), :] = jnp.broadcast_to(centre, (8, 128))
            for h in range(2):
                lanes = slice(128 * h, 128 * h + 128)
                y8[h, pl.ds(spot + 3, 8, stride=8), :] = jnp.ones((8, 128), f32)
                y8[h, pl.ds(spot + 4, 8, stride=8), :] = norm[:, lanes]
            return unused

        lax.fori_loop(0, MB // 8, one, 0, unroll=4)

    halves(own, 0)
    halves(other, MB)


def sample_tiles(own, other, table):
    return pl.pallas_call(
        sample_kernel,
        name="samples",
        out_shape=(
            jax.ShapeDtypeStruct((2, 2 * MB * 8, 128), f32),
            jax.ShapeDtypeStruct((MB, MP), f32),
        ),
        in_specs=[VMEM_SPEC] * 3,
        out_specs=(VMEM_SPEC,) * 2,
        scratch_shapes=[pltpu.VMEM((4, MB, MP), f32)],
    )(own, other, table)


def front(tile, y8, keep):
    wide = jnp.concatenate([tile, tile], axis=0)
    rows = lax.broadcasted_iota(jnp.int32, (8, 128), 0)
    centre = pltpu.roll(y8[:, :128], 3, 0)
    xs = jnp.where(rows < 3, (wide - centre) * SCALE, 0.0)
    norm = -0.5 * jnp.sum(xs * xs, axis=0, keepdims=True)
    weight = wide[3:4]
    x8 = jnp.where(rows == 3, norm, jnp.where(rows == 4, 1.0, xs))
    x1 = narrow(x8)
    x2 = narrow(x8 - x1)
    x3 = x8 - x1 - x2
    y1 = narrow(y8)
    y2 = narrow(y8 - y1)
    y3 = y8 - y1 - y2
    left = jnp.concatenate([x1, x1, x2, x2, x1, x3], axis=0).astype(bf16)
    lead = jnp.concatenate([y1, y2], axis=0).astype(bf16)
    tail = jnp.concatenate([y3, y1], axis=0).astype(bf16)
    right = jnp.concatenate([lead, lead, tail], axis=0)
    gauss = jnp.exp2(dot(left, right, 0, 0))
    high = gauss.astype(bf16)
    low = ((gauss - high.astype(f32)) * LIFT).astype(fp8)
    ax = x8 * (weight * keep)
    ax1 = narrow(ax)
    ax2 = jnp.concatenate([ax1, ax - ax1], axis=0).astype(bf16)
    ax8 = jnp.concatenate([ax] * 4, axis=0).astype(fp8)
    lead8 = jnp.concatenate([y8] * 4, axis=0).astype(fp8)
    return high, low, ax2, ax8, lead, lead8, xs, jnp.broadcast_to(weight * GAIN, (8, 128))


PIECES = 8
LIFT = 65536.0


def force_kernel(size, core, tiles, y8_hbm, force, own, other, y8, acc, rows, meta, sems, entries, *buffers):
    load_y8 = pltpu.make_async_copy(y8_hbm, y8, sems.at[1])
    load_y8.start()

    def row_of(peer, unused):
        rows[pl.ds(peer, 1), :] = tiles[peer, 2 * size, 0:1, :].astype(jnp.int32)
        return unused

    lax.fori_loop(0, PEERS, row_of, 0, unroll=8)
    lane = lax.broadcasted_iota(jnp.int32, (PEERS, 128), 1)
    chip = lax.broadcasted_iota(jnp.int32, (PEERS, 128), 0)
    mine = core[0]
    half = jnp.where(lane < size, mine, 1 - mine)
    sent = rows[...]
    rows[...] = jnp.where(
        lane < 2 * size, (half * MB + sent) * 1024 + chip * 16 + lane, sent
    )
    load_meta = pltpu.make_async_copy(rows, meta, sems.at[0])
    load_meta.start()
    acc[...] = jnp.zeros_like(acc)
    load_meta.wait()

    def list_peer(peer, count):
        for half in range(2):
            for c in range(size):
                entries[count + c] = meta[peer, half * size + c]
            count = count + meta[peer, 2 * size + half]
        return count

    total = lax.fori_loop(0, PEERS, list_peer, jnp.int32(0), unroll=2)
    last = entries[jnp.maximum(total - 1, 0)]
    for k in range(SPARE):
        entries[total + k] = last | (1 << 20)
    trips = (total + TRIP - 1) // TRIP

    load_y8.wait()

    def unpack(index):
        entry = entries[index]
        return (entry >> 4) & 63, entry & 15, (entry >> 10) & 511, entry >> 20

    def stage_front(index, place):
        peer, c, block, extra = unpack(index)
        keep = (1 - extra).astype(f32)
        at = pl.ds(pl.multiple_of(block * 8, 8), 8)
        samples = jnp.concatenate([y8[0, at, :], y8[1, at, :]], axis=1)
        values = front(tiles[peer, c], samples, keep)
        for k in range(PIECES):
            buffers[place * PIECES + k][...] = values[k]

    def stage_back(index, place):
        peer, c, block, _ = unpack(index)
        high, low, ax2, ax8, lead, lead8, xs, scale = [
            buffers[place * PIECES + k][...] for k in range(PIECES)
        ]
        q = dot(ax2, high, 1, 0)
        f = dot(lead, high, 1, 1)
        q = q[0:8] + q[8:16] + dot(ax8, low, 1, 0)[0:8] * (1.0 / LIFT)
        f = f[0:8] + f[8:16] + dot(lead8, low, 1, 1)[0:8] * (1.0 / LIFT)
        f = scale * (xs * f[3:4] - f)
        force[peer, pl.ds(c * 3, 3), :] = f[0:3]
        at = pl.ds(pl.multiple_of(block * 8, 8), 8)
        for h in range(2):
            acc[h, at, :] = acc[h, at, :] + q[:, 128 * h : 128 * h + 128]

    for u in range(LAG):
        stage_front(u, u)

    def trip(i, unused):
        for u in range(TRIP):
            stage_front(i * TRIP + u + LAG, (u + LAG) % RING)
            stage_back(i * TRIP + u, u % RING)
        return unused

    lax.fori_loop(0, trips, trip, 0)

    def finish(out, first):
        def one(i, unused):
            spot = (first + i * 8) * 8
            at = pl.ds(pl.multiple_of(i * 8, 8), 8)
            for h in range(2):
                amount = acc[h, pl.ds(spot + 4, 8, stride=8), :]
                for k in range(3):
                    rows = pl.ds(spot + k, 8, stride=8)
                    out[k, at, 128 * h : 128 * h + 128] = (y8[h, rows, :] * amount - acc[h, rows, :]) * GAIN
            return unused

        lax.fori_loop(0, MB // 8, one, 0, unroll=4)

    finish(own, 0)
    finish(other, MB)


def forces(size, core, tiles, y8):
    one = [
        pltpu.VMEM((QP, MP), bf16),
        pltpu.VMEM((QP, MP), fp8),
        pltpu.VMEM((16, QP), bf16),
        pltpu.VMEM((32, QP), fp8),
        pltpu.VMEM((16, MP), bf16),
        pltpu.VMEM((32, MP), fp8),
        pltpu.VMEM((8, QP), f32),
        pltpu.VMEM((8, QP), f32),
    ]
    part = jax.ShapeDtypeStruct((3, MB, MP), f32)
    return pl.pallas_call(
        functools.partial(force_kernel, size),
        name="forces",
        out_shape=(jax.ShapeDtypeStruct((PEERS, force_rows(size), QP), f32), part, part),
        in_specs=[SMEM_SPEC, VMEM_SPEC, ANY_SPEC],
        out_specs=(VMEM_SPEC,) * 3,
        scratch_shapes=[
            pltpu.VMEM(y8.shape, f32),
            pltpu.VMEM(y8.shape, f32),
            pltpu.VMEM((PEERS, 128), jnp.int32),
            pltpu.SMEM((PEERS, 128), jnp.int32),
            pltpu.SemaphoreType.DMA((2,)),
            pltpu.SMEM((2 * PEERS * size + CAP + SPARE,), jnp.int32),
        ]
        + one * RING,
    )(core, tiles, y8)


def force_rows(size):
    return -(-6 * size // 8) * 8


def gather_kernel(low, size, ps, cnt, force, out, even, odd):
    even[...] = jnp.zeros_like(even)
    odd[...] = jnp.zeros_like(odd)

    def one_peer(peer, unused):
        for half in range(2):
            owner = 2 * peer + half
            live = cnt[owner] - low
            for c in range(size):
                block = jnp.where(c < live, ps[peer * (2 * CAP) + half * CAP + low + c], SB)
                row = 3 * (half * size + c)
                total = odd if (half * size + c) % 2 else even
                total[block] = total[block] + force[peer, row : row + 3, :]
        return unused

    lax.fori_loop(0, PEERS, one_peer, 0, unroll=2)
    out[...] = even[0:SB] + odd[0:SB]


def gather_forces(low, size, ps, cnt, force):
    return pl.pallas_call(
        functools.partial(gather_kernel, low, size),
        name="gather",
        out_shape=jax.ShapeDtypeStruct((SB, 3, QP), f32),
        in_specs=[SMEM_SPEC] * 2 + [VMEM_SPEC],
        out_specs=VMEM_SPEC,
        scratch_shapes=[pltpu.VMEM((SB + 1, 3, QP), f32)] * 2,
    )(ps, cnt, force)


def exchange(x):
    return lax.all_to_all(x, ("gx", "g"), split_axis=0, concat_axis=0, tiled=True)


def swap(x):
    return lax.ppermute(x, "core", [(0, 1), (1, 0)])


def body(slave_coords, slave_weight, master_ctrl, master_wt, pair_slave, pair_master, pair_count):
    coords = slave_coords.reshape(3, SB, QP).transpose(1, 0, 2)
    payload = pack(
        CAP, pair_slave, pair_master, pair_count, coords, slave_weight.reshape(SB, QP)
    )
    tiles = exchange(payload)

    blocks = jnp.concatenate([master_ctrl, master_wt[None, :]], axis=0).reshape(4, MB, MP)
    table = spread_table()
    y8, total = sample_tiles(blocks, swap(blocks), table)

    core = lax.axis_index("core").reshape(1).astype(jnp.int32)
    tiles = pltpu.with_memory_space_constraint(tiles, pltpu.VMEM)
    force, q, away = forces(CAP, core, tiles, y8)
    force = exchange(force)
    away = swap(away)
    slave_force = gather_forces(
        0, CAP, pair_slave, pair_count, pltpu.with_memory_space_constraint(force, pltpu.VMEM)
    )

    q = (q + away) / total
    master_force = (
        jnp.einsum("cbj,jk->cbk", q, table, precision=lax.Precision.HIGHEST) * blocks[3:]
    )
    return (
        slave_force.transpose(1, 0, 2).reshape(3, SB * QP),
        master_force.reshape(3, MB * MP),
    )


def solution(mesh):
    split = Mesh(mesh.devices.reshape(4, 16, 2), ("gx", "g", "core"))
    every = ("gx", "g", "core")
    wide, flat = P(None, every), P(every)
    return jax.shard_map(
        body,
        mesh=split,
        in_specs=(wide, flat, wide, flat, flat, flat, flat),
        out_specs=(wide, wide),
        check_vma=False,
    )
```

```python
import functools
import math

import jax
import jax.numpy as jnp
import numpy as np
from jax import lax
from jax.experimental import pallas as pl
from jax.experimental.pallas import tpu as pltpu
from jax.sharding import Mesh
from jax.sharding import PartitionSpec as P


QP = 128
CAP = 5
SB = 512
MB = 256
MP = 256
PEERS = 64
TRIP = 32
LAG = 4
RING = 8
SPARE = TRIP + LAG

f32 = jnp.float32
bf16 = jnp.bfloat16
fp8 = jnp.float8_e4m3fn
SCALE = math.sqrt(2.0 * math.log2(math.e) / 3.0)
GAIN = 0.01 / SCALE

VMEM_SPEC = pl.BlockSpec(memory_space=pltpu.VMEM)
ANY_SPEC = pl.BlockSpec(memory_space=pl.ANY)
SMEM_SPEC = pl.BlockSpec(memory_space=pltpu.SMEM)


def bezier_table():
    params = (np.arange(4) + 0.5) / 4.0
    powers = np.arange(4)
    binomial = np.array([1.0, 3.0, 3.0, 1.0])
    bernstein = (
        binomial[None, :]
        * params[:, None] ** powers[None, :]
        * (1.0 - params[:, None]) ** (3.0 - powers[None, :])
    )
    return (bernstein[:, None, :, None] * bernstein[None, :, None, :]).reshape(16, 16)


def spread_table():
    return jnp.asarray(np.kron(np.eye(16), bezier_table()).astype(np.float32))


def dot(a, b, left, right):
    return lax.dot_general(a, b, (((left,), (right,)), ((), ())), preferred_element_type=f32)


def narrow(x):
    return x.astype(bf16).astype(f32)


def pack_kernel(size, ps, pm, cnt, coords, weight, out, built, sems):
    lane = lax.broadcasted_iota(jnp.int32, (1, 128), 1)
    share = PEERS // PARTS

    def one_peer(peer, unused):
        row = jnp.zeros((1, 128), jnp.int32)
        for spot in range(2 * size):
            slot = peer * (2 * size) + spot
            block = ps[slot]
            built[peer, spot, 0:3, :] = coords[block]
            built[peer, spot, 3:4, :] = weight[pl.ds(block, 1), :]
            row = jnp.where(lane == spot, pm[slot], row)
        for owner in range(2):
            row = jnp.where(lane == 2 * size + owner, cnt[2 * peer + owner], row)
        built[peer, 2 * size, 0:1, :] = row.astype(f32)
        return unused

    copies = []
    for part in range(PARTS):
        lax.fori_loop(part * share, (part + 1) * share, one_peer, 0, unroll=2)
        some = pl.ds(part * share, share)
        copies.append(pltpu.make_async_copy(built.at[some], out.at[some], sems.at[part]))
        copies[-1].start()
    for copy in copies:
        copy.wait()


PARTS = 4


def pack(size, ps, pm, cnt, coords, weight):
    shape = (PEERS, 2 * size + 1, 4, QP)
    return pl.pallas_call(
        functools.partial(pack_kernel, size),
        name="pack",
        out_shape=jax.ShapeDtypeStruct(shape, f32),
        in_specs=[SMEM_SPEC] * 3 + [VMEM_SPEC] * 2,
        out_specs=ANY_SPEC,
        scratch_shapes=[pltpu.VMEM(shape, f32), pltpu.SemaphoreType.DMA((PARTS,))],
    )(ps, pm, cnt, coords, weight)


def sample_kernel(own, other, table, y8, total, sums):
    def halves(source, base):
        def lift(k, unused):
            rows = source[k] * jnp.where(k == 3, 1.0, source[3])
            sums[k] = lax.dot_general(
                rows,
                table[...],
                (((1,), (1,)), ((), ())),
                precision=lax.Precision.HIGHEST,
                preferred_element_type=f32,
            )
            return unused

        lax.fori_loop(0, 4, lift, 0)
        if base == 0:
            total[...] = sums[3]

        def one(i, unused):
            at = pl.ds(pl.multiple_of(i * 8, 8), 8)
            inverse = 1.0 / sums[3, at, :]
            norm = jnp.zeros((8, MP), f32)
            spot = (base + i * 8) * 8
            for k in range(3):
                y = sums[k, at, :] * inverse
                centre = jnp.sum(y, axis=1, keepdims=True) * (1.0 / MP)
                y = (y - centre) * SCALE
                norm = norm - 0.5 * (y * y)
                for h in range(2):
                    lanes = slice(128 * h, 128 * h + 128)
                    y8[h, pl.ds(spot + k, 8, stride=8), :] = y[:, lanes]
                    y8[h, pl.ds(spot + 5 + k, 8, stride=8), :] = jnp.broadcast_to(centre, (8, 128))
            for h in range(2):
                lanes = slice(128 * h, 128 * h + 128)
                y8[h, pl.ds(spot + 3, 8, stride=8), :] = jnp.ones((8, 128), f32)
                y8[h, pl.ds(spot + 4, 8, stride=8), :] = norm[:, lanes]
            return unused

        lax.fori_loop(0, MB // 8, one, 0, unroll=4)

    halves(own, 0)
    halves(other, MB)


def sample_tiles(own, other, table):
    return pl.pallas_call(
        sample_kernel,
        name="samples",
        out_shape=(
            jax.ShapeDtypeStruct((2, 2 * MB * 8, 128), f32),
            jax.ShapeDtypeStruct((MB, MP), f32),
        ),
        in_specs=[VMEM_SPEC] * 3,
        out_specs=(VMEM_SPEC,) * 2,
        scratch_shapes=[pltpu.VMEM((4, MB, MP), f32)],
    )(own, other, table)


def front(tile, y8, keep):
    wide = jnp.concatenate([tile, tile], axis=0)
    rows = lax.broadcasted_iota(jnp.int32, (8, 128), 0)
    centre = pltpu.roll(y8[:, :128], 3, 0)
    xs = jnp.where(rows < 3, (wide - centre) * SCALE, 0.0)
    norm = -0.5 * jnp.sum(xs * xs, axis=0, keepdims=True)
    weight = wide[3:4]
    x8 = jnp.where(rows == 3, norm + SHIFT, jnp.where(rows == 4, 1.0, xs))
    x1 = narrow(x8)
    x2 = narrow(x8 - x1)
    x3 = x8 - x1 - x2
    y1 = narrow(y8)
    y2 = narrow(y8 - y1)
    y3 = y8 - y1 - y2
    left = jnp.concatenate([x1, x1, x2, x2, x1, x3], axis=0).astype(bf16)
    lead = jnp.concatenate([y1, y2], axis=0).astype(bf16)
    tail = jnp.concatenate([y3, y1], axis=0).astype(bf16)
    right = jnp.concatenate([lead, lead, tail], axis=0)
    gauss = jnp.exp2(dot(left, right, 0, 0))
    high = gauss.astype(bf16)
    low = (gauss - high.astype(f32)).astype(fp8)
    ax = x8 * (weight * keep)
    ax1 = narrow(ax)
    ax2 = jnp.concatenate([ax1, ax - ax1], axis=0).astype(bf16)
    ax8 = ax.astype(fp8)
    lead8 = y8.astype(fp8)
    return high, low, ax2, ax8, lead, lead8, xs, jnp.broadcast_to(weight * (GAIN / LIFT), (8, 128))


PIECES = 8
SHIFT = 16.0
LIFT = 2.0**SHIFT


def force_kernel(size, core, tiles, y8_hbm, force_hbm, own_hbm, other_hbm, force, own, other, y8, acc, rows, meta, sems, entries, *buffers):
    load_y8 = pltpu.make_async_copy(y8_hbm, y8, sems.at[1])
    load_y8.start()

    def row_of(peer, unused):
        rows[pl.ds(peer, 1), :] = tiles[peer, 2 * size, 0:1, :].astype(jnp.int32)
        return unused

    lax.fori_loop(0, PEERS, row_of, 0, unroll=8)
    lane = lax.broadcasted_iota(jnp.int32, (PEERS, 128), 1)
    chip = lax.broadcasted_iota(jnp.int32, (PEERS, 128), 0)
    mine = core[0]
    half = jnp.where(lane < size, mine, 1 - mine)
    sent = rows[...]
    rows[...] = jnp.where(
        lane < 2 * size, (half * MB + sent) * 1024 + chip * 16 + lane, sent
    )
    load_meta = pltpu.make_async_copy(rows, meta, sems.at[0])
    load_meta.start()
    acc[...] = jnp.zeros_like(acc)
    load_meta.wait()

    def list_peer(peer, count):
        for half in range(2):
            for c in range(size):
                entries[count + c] = meta[peer, half * size + c]
            count = count + meta[peer, 2 * size + half]
        return count

    total = lax.fori_loop(0, PEERS, list_peer, jnp.int32(0), unroll=2)
    last = entries[jnp.maximum(total - 1, 0)]
    for k in range(SPARE):
        entries[total + k] = last | (1 << 20)
    trips = (total + TRIP - 1) // TRIP

    load_y8.wait()

    def unpack(index):
        entry = entries[index]
        return (entry >> 4) & 63, entry & 15, (entry >> 10) & 511, entry >> 20

    def stage_front(index, place):
        peer, c, block, extra = unpack(index)
        keep = (1 - extra).astype(f32)
        at = pl.ds(pl.multiple_of(block * 8, 8), 8)
        samples = jnp.concatenate([y8[0, at, :], y8[1, at, :]], axis=1)
        values = front(tiles[peer, c], samples, keep)
        for k in range(PIECES):
            buffers[place * PIECES + k][...] = values[k]

    def stage_back(index, place):
        peer, c, block, _ = unpack(index)
        high, low, ax2, ax8, lead, lead8, xs, scale = [
            buffers[place * PIECES + k][...] for k in range(PIECES)
        ]
        q = dot(ax2, high, 1, 0)
        f = dot(lead, high, 1, 1)
        q = q[0:8] + q[8:16] + dot(ax8, low, 1, 0)
        f = f[0:8] + f[8:16] + dot(lead8, low, 1, 1)
        f = scale * (xs * f[3:4] - f)
        force[peer, pl.ds(c * 3, 3), :] = f[0:3]
        at = pl.ds(pl.multiple_of(block * 8, 8), 8)
        for h in range(2):
            acc[h, at, :] = acc[h, at, :] + q[:, 128 * h : 128 * h + 128]

    for u in range(LAG):
        stage_front(u, u)

    def trip(i, unused):
        for u in range(TRIP):
            stage_back(i * TRIP + u, u % RING)
            stage_front(i * TRIP + u + LAG, (u + LAG) % RING)
        return unused

    lax.fori_loop(0, trips, trip, 0)

    def finish(out, first):
        def one(i, unused):
            spot = (first + i * 8) * 8
            at = pl.ds(pl.multiple_of(i * 8, 8), 8)
            for h in range(2):
                amount = acc[h, pl.ds(spot + 4, 8, stride=8), :]
                for k in range(3):
                    rows = pl.ds(spot + k, 8, stride=8)
                    out[k, at, 128 * h : 128 * h + 128] = (y8[h, rows, :] * amount - acc[h, rows, :]) * (GAIN / LIFT)
            return unused

        lax.fori_loop(0, MB // 8, one, 0, unroll=4)

    copies = [
        pltpu.make_async_copy(force, force_hbm, sems.at[2]),
        pltpu.make_async_copy(other, other_hbm, sems.at[3]),
        pltpu.make_async_copy(own, own_hbm, sems.at[4]),
    ]
    copies[0].start()
    finish(other, MB)
    copies[1].start()
    finish(own, 0)
    copies[2].start()
    for copy in copies:
        copy.wait()


def forces(size, core, tiles, y8):
    one = [
        pltpu.VMEM((QP, MP), bf16),
        pltpu.VMEM((QP, MP), fp8),
        pltpu.VMEM((16, QP), bf16),
        pltpu.VMEM((8, QP), fp8),
        pltpu.VMEM((16, MP), bf16),
        pltpu.VMEM((8, MP), fp8),
        pltpu.VMEM((8, QP), f32),
        pltpu.VMEM((8, QP), f32),
    ]
    part = jax.ShapeDtypeStruct((3, MB, MP), f32)
    return pl.pallas_call(
        functools.partial(force_kernel, size),
        name="forces",
        out_shape=(jax.ShapeDtypeStruct((PEERS, force_rows(size), QP), f32), part, part),
        in_specs=[SMEM_SPEC, VMEM_SPEC, ANY_SPEC],
        out_specs=(ANY_SPEC,) * 3,
        scratch_shapes=[
            pltpu.VMEM((PEERS, force_rows(size), QP), f32),
            pltpu.VMEM((3, MB, MP), f32),
            pltpu.VMEM((3, MB, MP), f32),
            pltpu.VMEM(y8.shape, f32),
            pltpu.VMEM(y8.shape, f32),
            pltpu.VMEM((PEERS, 128), jnp.int32),
            pltpu.SMEM((PEERS, 128), jnp.int32),
            pltpu.SemaphoreType.DMA((5,)),
            pltpu.SMEM((2 * PEERS * size + CAP + SPARE,), jnp.int32),
        ]
        + one * RING,
    )(core, tiles, y8)


def force_rows(size):
    return -(-6 * size // 8) * 8


def gather_kernel(low, size, ps, cnt, force, out, even, odd, sems):
    even[...] = jnp.zeros_like(even)
    odd[...] = jnp.zeros_like(odd)

    def one_peer(peer, unused):
        for half in range(2):
            owner = 2 * peer + half
            live = cnt[owner] - low
            for c in range(size):
                block = jnp.where(c < live, ps[peer * (2 * CAP) + half * CAP + low + c], SB)
                row = 3 * (half * size + c)
                total = odd if (half * size + c) % 2 else even
                total[block] = total[block] + force[peer, row : row + 3, :]
        return unused

    lax.fori_loop(0, PEERS, one_peer, 0, unroll=2)
    copies = []
    for part in range(PARTS):
        some = pl.ds(part * (SB // PARTS), SB // PARTS)
        even[some] = even[some] + odd[some]
        copies.append(pltpu.make_async_copy(even.at[some], out.at[some], sems.at[part]))
        copies[-1].start()
    for copy in copies:
        copy.wait()


def gather_forces(low, size, ps, cnt, force):
    return pl.pallas_call(
        functools.partial(gather_kernel, low, size),
        name="gather",
        out_shape=jax.ShapeDtypeStruct((SB, 3, QP), f32),
        in_specs=[SMEM_SPEC] * 2 + [VMEM_SPEC],
        out_specs=ANY_SPEC,
        scratch_shapes=[pltpu.VMEM((SB + 1, 3, QP), f32)] * 2 + [pltpu.SemaphoreType.DMA((PARTS,))],
    )(ps, cnt, force)


def exchange(x):
    return lax.all_to_all(x, ("gx", "g"), split_axis=0, concat_axis=0, tiled=True)


def swap(x):
    return lax.ppermute(x, "core", [(0, 1), (1, 0)])


def body(slave_coords, slave_weight, master_ctrl, master_wt, pair_slave, pair_master, pair_count):
    coords = slave_coords.reshape(3, SB, QP).transpose(1, 0, 2)
    payload = pack(
        CAP, pair_slave, pair_master, pair_count, coords, slave_weight.reshape(SB, QP)
    )
    tiles = exchange(payload)

    blocks = jnp.concatenate([master_ctrl, master_wt[None, :]], axis=0).reshape(4, MB, MP)
    table = spread_table()
    y8, total = sample_tiles(blocks, swap(blocks), table)

    core = lax.axis_index("core").reshape(1).astype(jnp.int32)
    tiles = pltpu.with_memory_space_constraint(tiles, pltpu.VMEM)
    force, q, away = forces(CAP, core, tiles, y8)
    force = exchange(force)
    away = swap(away)
    slave_force = gather_forces(
        0, CAP, pair_slave, pair_count, pltpu.with_memory_space_constraint(force, pltpu.VMEM)
    )

    q = (q + away) / total
    master_force = (
        jnp.einsum("cbj,jk->cbk", q, table, precision=lax.Precision.HIGHEST) * blocks[3:]
    )
    return (
        slave_force.transpose(1, 0, 2).reshape(3, SB * QP),
        master_force.reshape(3, MB * MP),
    )


def solution(mesh):
    split = Mesh(mesh.devices.reshape(4, 16, 2), ("gx", "g", "core"))
    every = ("gx", "g", "core")
    wide, flat = P(None, every), P(every)
    return jax.shard_map(
        body,
        mesh=split,
        in_specs=(wide, flat, wide, flat, flat, flat, flat),
        out_specs=(wide, wide),
        check_vma=False,
    )
```
